32 devices in a mesh: space: 4 (over y, x), snap: 8 (over z, core).
Axes of the slice: x: 2, y: 2, z: 4, core: 2. Of those that a mesh axis runs over, the one named last changes fastest.
Arguments:
- snapshots: bfloat16 [4096, 32768], P('space', 'snap'), may hold values from -6 to 6
- vectors_cyclic: float32 [32768, 64], P('snap', 'space'), may hold values from -0.03125 to 0.03125
- eigen_values: float32 [64], replicated, may hold values from 0.25 to 25
- held_out: bfloat16 [4096, 256], P(('space', 'snap')), may hold values from -6 to 6
Outputs:
- modes: bfloat16 [4096, 64], P(('space', 'snap'))
- coefficients: float32 [64, 256], replicated
The draws below stay inside these ranges and needn't reach their ends.
All inputs are finite; a program needn't handle non-finite values.
Results may differ from the reference program's by a relative error of at most 0.0052.
Values sent between devices are 32-bit elements; how exact they have to be, the bound alone decides.
No kernel may reach another device: no remote copies, remote signals or barrier semaphores. Data moves between devices by JAX's collectives and lax.ppermute only.
A program may use at most 64 MiB of HBM per device.

```python
import math
import jax
import jax.numpy as jnp
from jax import lax

MODES = 64
SNAP_DEV = 4096
HELD = 256
ROW_BLOCK = 16
COL_BLOCK = 4
CELLS = 4096
SNAPS = 32768
N_SPACE = 4
N_SNAP = 8


def raised(entries, rng, source, target, blocks, factor):
    def block_of(dim):
        return (jnp.arange(entries.shape[dim]) // (entries.shape[dim] // blocks)).reshape((-1,) + (1,) * (entries.ndim - 1 - dim))

    one_side = jax.random.permutation(rng, blocks)[block_of(target)]
    second = (block_of(target) + blocks // 2) % blocks
    return jnp.where((block_of(source) == one_side) | (block_of(source) == second), factor * entries, entries)


def steps_of(key, dims, pieces, low, largest):
    factor_of, own = 1.0, jax.random.fold_in(key, 6)
    for axis_at, blocks in pieces:
        steps = jnp.exp(jax.random.uniform(jax.random.fold_in(own, axis_at), (blocks,), jnp.float32, low / len(pieces), largest / len(pieces)))
        factor_of = factor_of * jnp.repeat(steps, dims[axis_at] // blocks).reshape([-1 if axis == axis_at else 1 for axis in range(len(dims))])
    return factor_of


def noise(stream_key, shape, scale, bound, split=(), held_as=jnp.bfloat16):
    gain = steps_of(stream_key, shape, split, -0.22, 0.18) if split else 1.0
    values = jax.random.normal(stream_key, shape, jnp.float32) * scale * gain
    return jnp.minimum(jnp.maximum(values, -bound), bound).astype(held_as)


def heavy_noise(key, dims, spread, reach, split, heavy, kind=jnp.bfloat16):
    result = spread * jax.random.normal(key, dims, jnp.float32)
    if split:
        result = result * steps_of(key, dims, split, -0.22, 0.18)
    return jnp.clip(raised(result, jax.random.fold_in(key, 3), *heavy), -reach, reach).astype(kind)


def setup_inputs(seed: int = 0) -> dict:
    key_of = jax.random.split(jax.random.key(seed), 5)
    snapshots = heavy_noise(key_of[0], (CELLS, SNAPS), 1.0, 6.0, ((0, 4), (1, 8)), (1, 0, 8, 2.0))
    vectors_cyclic = noise(key_of[1], (SNAPS, MODES), SNAPS ** -0.5, 0.03125, ((0, 8), (1, 4)), jnp.float32)
    eigen_values = jnp.clip(jnp.exp(jax.random.uniform(key_of[2], (MODES,), jnp.float32, math.log(0.25), math.log(25.0))), 0.25, 25.0)
    held_out = noise(key_of[3], (CELLS, HELD), 1.0, 6.0, ((0, 32),))
    return dict(snapshots=snapshots, vectors_cyclic=vectors_cyclic, eigen_values=eigen_values, held_out=held_out)


def reference(snapshots, vectors_cyclic, eigen_values, held_out):
    eigvec = vectors_cyclic.reshape(N_SNAP, SNAP_DEV // ROW_BLOCK, ROW_BLOCK, MODES)
    eigvec = eigvec.transpose(1, 0, 2, 3).reshape(SNAPS, MODES)
    eigvec = eigvec.reshape(SNAPS, N_SPACE, MODES // (N_SPACE * COL_BLOCK), COL_BLOCK)
    eigvec = eigvec.transpose(0, 2, 1, 3).reshape(SNAPS, MODES)
    scaled = (eigvec * lax.rsqrt(eigen_values)[None, :]).astype(jnp.bfloat16)
    modes = jnp.dot(snapshots, scaled, preferred_element_type=jnp.float32).astype(jnp.bfloat16)
    coefficients = lax.dot_general(modes, held_out, (((0,), (0,)), ((), ())), preferred_element_type=jnp.float32)
    coefficients = coefficients / math.sqrt(CELLS)
    return (modes, coefficients)
```

```python
import math

import jax
import jax.numpy as jnp
from jax import lax
from jax.experimental import pallas as pl
from jax.experimental.pallas import tpu as pltpu
from jax.sharding import PartitionSpec as P

ROW_BLOCK = 16
COL_BLOCK = 4
LANES = 128
GROUPS = LANES // ROW_BLOCK
VMEM = pltpu.VMEM
SMEM_SPEC = pl.BlockSpec(memory_space=pltpu.SMEM)
VMEM_SPEC = pl.BlockSpec(memory_space=pltpu.VMEM)


def swap(value, axis, mask):
    count = lax.axis_size(axis)
    return lax.ppermute(value, axis, [(i, i ^ mask) for i in range(count)])


def tree_sum(terms):
    while len(terms) > 1:
        terms = [terms[i] + terms[i + 1] for i in range(0, len(terms), 2)]
    return terms[0]


def split_kernel(space_count, pos_ref, own_ref, other_ref, eig_ref, *out_refs):
    p, q = pos_ref[0], pos_ref[1]
    width = own_ref.shape[0]
    chunk = out_refs[0].shape[2]
    row = lax.broadcasted_iota(jnp.int32, (width, eig_ref.shape[1]), 0)
    mode = lax.broadcasted_iota(jnp.int32, (width, eig_ref.shape[1]), 1)
    mine = (row // COL_BLOCK * space_count + q) * COL_BLOCK + row % COL_BLOCK
    picked = jnp.where(mode == mine, eig_ref[...], 0.0)
    scale = lax.rsqrt(jnp.sum(picked, axis=1, keepdims=True))
    for d, out_ref in enumerate(out_refs):
        start = pl.multiple_of((p ^ (2 * d)) * chunk, LANES)
        out_ref[0] = own_ref[:, pl.ds(start, chunk)] * scale
        out_ref[1] = other_ref[:, pl.ds(start, chunk)] * scale


def split_pieces(pos, own, other, eig, snap_count, space_count):
    width, rows = own.shape
    chunk = rows // snap_count
    piece = jax.ShapeDtypeStruct((2, width, chunk), jnp.float32)
    return pl.pallas_call(
        lambda *refs: split_kernel(space_count, *refs),
        out_shape=[piece] * (snap_count // 2),
        in_specs=[SMEM_SPEC, VMEM_SPEC, VMEM_SPEC, VMEM_SPEC],
        out_specs=[VMEM_SPEC] * (snap_count // 2),
        name="split_pieces",
    )(pos, own, other, eig)


def interleave(blocks):
    lane = lax.broadcasted_iota(jnp.int32, blocks[0].shape, 1) // ROW_BLOCK
    step = 1
    while step < GROUPS:
        high = (lane & step) != 0
        mixed = list(blocks)
        for a in range(GROUPS):
            if a & step == 0:
                b = a | step
                low_of_b = pltpu.roll(blocks[b], step * ROW_BLOCK, 1)
                high_of_a = pltpu.roll(blocks[a], LANES - step * ROW_BLOCK, 1)
                mixed[a] = jnp.where(high, low_of_b, blocks[a])
                mixed[b] = jnp.where(high, blocks[b], high_of_a)
        blocks = mixed
        step *= 2
    return blocks


def multiply_kernel(pos_ref, *refs):
    parts, (snap_ref, keep_ref, send_ref, scaled_ref, cells_ref) = refs[:-5], refs[-5:]
    p = pos_ref[0]
    snap_count, width, chunk = parts[0].shape
    groups_of_p = snap_count // GROUPS
    for e, part in enumerate(parts):
        for outer in range(groups_of_p):
            slots = [p ^ (outer * GROUPS + g) for g in range(GROUPS)]
            for t in range(chunk // LANES):
                blocks = [part[slot, :, t * LANES : (t + 1) * LANES] for slot in slots]
                for j, block in enumerate(interleave(blocks)):
                    tile = (t * GROUPS + j) * groups_of_p + outer
                    scaled_ref[e * width : (e + 1) * width, tile * LANES : (tile + 1) * LANES] = block.astype(
                        jnp.bfloat16
                    )
    cells = cells_ref.shape[2]
    total = lax.dot_general(
        scaled_ref[...], snap_ref[...], (((1,), (1,)), ((), ())), preferred_element_type=jnp.float32
    )
    for owner in range(snap_count):
        cells_ref[owner] = total[:, owner * cells : (owner + 1) * cells]
    for d in range(snap_count // 2):
        keep_ref[d] = cells_ref[p ^ (2 * d)]
        send_ref[d] = cells_ref[p ^ (2 * d + 1)]


def multiply(pos, parts, snapshots):
    snap_count, width, chunk = parts[0].shape
    cells, depth = snapshots.shape
    modes = width * len(parts)
    half = jax.ShapeDtypeStruct((snap_count // 2, modes, cells // snap_count), jnp.float32)
    return pl.pallas_call(
        multiply_kernel,
        out_shape=[half, half],
        in_specs=[SMEM_SPEC] + [VMEM_SPEC] * (len(parts) + 1),
        out_specs=[VMEM_SPEC, VMEM_SPEC],
        scratch_shapes=[
            VMEM((modes, depth), jnp.bfloat16),
            VMEM((snap_count, modes, cells // snap_count), jnp.float32),
        ],
        name="multiply",
    )(pos, *parts, snapshots)


def project_kernel(width, pos_ref, *refs):
    sums, (held_ref, modes_ref, keep_ref, send_ref, coef_ref) = refs[:-5], refs[-5:]
    p, q = pos_ref[0], pos_ref[1]
    rounded = tree_sum([ref[...] for ref in sums]).astype(jnp.bfloat16)
    modes = rounded.shape[0]
    space_count = modes // width
    target = lax.broadcasted_iota(jnp.int32, (modes, modes), 0)
    source = lax.broadcasted_iota(jnp.int32, (modes, modes), 1)
    e, r = source // width, source % width
    mode = (r // COL_BLOCK * space_count + (q ^ e)) * COL_BLOCK + r % COL_BLOCK
    order = jnp.where(mode == target, 1.0, 0.0).astype(jnp.bfloat16)
    ordered = jnp.dot(order, rounded, preferred_element_type=jnp.float32).astype(jnp.bfloat16)
    modes_ref[...] = ordered
    coef_ref[...] = jnp.dot(ordered, held_ref[...], preferred_element_type=jnp.float32)
    half = modes // 2
    core = p & 1
    keep_ref[...] = coef_ref[pl.ds(pl.multiple_of(core * half, 8), half), :]
    send_ref[...] = coef_ref[pl.ds(pl.multiple_of((1 - core) * half, 8), half), :]


def project(pos, sums, held, width):
    modes, cells = sums[0].shape
    count = held.shape[1]
    half = jax.ShapeDtypeStruct((modes // 2, count), jnp.float32)
    return pl.pallas_call(
        lambda *refs: project_kernel(width, *refs),
        out_shape=[jax.ShapeDtypeStruct((modes, cells), jnp.bfloat16), half, half],
        in_specs=[SMEM_SPEC] + [VMEM_SPEC] * (len(sums) + 1),
        out_specs=[VMEM_SPEC] * 3,
        scratch_shapes=[VMEM((modes, count), jnp.float32)],
        name="project",
    )(pos, *sums, held)


def per_device(snapshots, vectors_cyclic, eigen_values, held_out):
    snap_count = lax.axis_size("snap")
    space_count = lax.axis_size("space")
    p, q = lax.axis_index("snap"), lax.axis_index("space")
    pos = jnp.stack([p, q]).astype(jnp.int32)
    distances = range(1, snap_count // 2)
    width = vectors_cyclic.shape[1]

    own = vectors_cyclic.T
    other = swap(own, "snap", 1)
    pieces = split_pieces(pos, own, other, eigen_values[None, :], snap_count, space_count)
    pieces = [pieces[0]] + [swap(pieces[d], "snap", 2 * d) for d in distances]
    slab = jnp.concatenate(pieces)
    parts = [slab] + [swap(slab, "space", e) for e in range(1, space_count)]

    keep, send = multiply(pos, parts, snapshots)
    paired = keep + swap(send, "snap", 1)
    sums = [paired[0]] + [swap(paired[d], "snap", 2 * d) for d in distances]

    modes, keep, send = project(pos, sums, held_out, width)
    half = keep + swap(send, "snap", 1)
    half = tree_sum([half] + [swap(half, "snap", 2 * d) for d in distances])
    half = tree_sum([half] + [swap(half, "space", e) for e in range(1, space_count)])
    far = swap(half, "snap", 1)
    first = p % 2 == 0
    coefficients = jnp.concatenate([jnp.where(first, half, far), jnp.where(first, far, half)])
    total_cells = snapshots.shape[0] * space_count
    return (modes.T, coefficients / math.sqrt(total_cells))


def solution(mesh):
    return jax.shard_map(
        per_device,
        mesh=mesh,
        in_specs=(P("space", "snap"), P("snap", "space"), P(), P(("space", "snap"), None)),
        out_specs=(P(("space", "snap"), None), P()),
        check_vma=False,
    )
```

```python
import math

import jax
import jax.numpy as jnp
from jax import lax
from jax.experimental import pallas as pl
from jax.experimental.pallas import tpu as pltpu
from jax.sharding import PartitionSpec as P

ROW_BLOCK = 16
COL_BLOCK = 4
LANES = 128
SUBLANES = 8
GROUPS = LANES // ROW_BLOCK
MIB = 1 << 20
IN_SMEM = pl.BlockSpec(memory_space=pltpu.SMEM)
IN_VMEM = pl.BlockSpec(memory_space=pltpu.VMEM)
IN_HBM = pl.BlockSpec(memory_space=pltpu.HBM)


def params(mib):
    return pltpu.CompilerParams(vmem_limit_bytes=mib * MIB)


def swap(value, axis, mask):
    count = lax.axis_size(axis)
    return lax.ppermute(value, axis, [(i, i ^ mask) for i in range(count)])


def tree_sum(terms):
    while len(terms) > 1:
        terms = [terms[i] + terms[i + 1] for i in range(0, len(terms), 2)]
    return terms[0]


def widen_kernel(pos_ref, held_ref, keep_ref, send_ref):
    half = keep_ref.shape[1]
    core = pos_ref[0] & 1
    keep_ref[...] = held_ref[:, pl.ds(pl.multiple_of(core * half, LANES), half)].astype(jnp.float32)
    send_ref[...] = held_ref[:, pl.ds(pl.multiple_of((1 - core) * half, LANES), half)].astype(jnp.float32)


def widen(pos, held):
    rows, columns = held.shape
    half = jax.ShapeDtypeStruct((rows, columns // 2), jnp.float32)
    return pl.pallas_call(
        widen_kernel,
        out_shape=[half, half],
        in_specs=[IN_SMEM, IN_VMEM],
        out_specs=[IN_VMEM, IN_VMEM],
        compiler_params=params(2),
        name="widen",
    )(pos, held)


def split_kernel(space_count, pos_ref, own_ref, other_ref, eig_ref, *out_refs):
    p, q = pos_ref[0], pos_ref[1]
    width = own_ref.shape[0]
    chunk = out_refs[0].shape[2]
    row = lax.broadcasted_iota(jnp.int32, (width, eig_ref.shape[1]), 0)
    mode = lax.broadcasted_iota(jnp.int32, (width, eig_ref.shape[1]), 1)
    mine = (row // COL_BLOCK * space_count + q) * COL_BLOCK + row % COL_BLOCK
    picked = jnp.where(mode == mine, eig_ref[...], 0.0)
    scale = lax.rsqrt(jnp.sum(picked, axis=1, keepdims=True))
    for d, out_ref in enumerate(out_refs):
        start = pl.multiple_of((p ^ (2 * d)) * chunk, LANES)
        out_ref[0] = own_ref[:, pl.ds(start, chunk)] * scale
        out_ref[1] = other_ref[:, pl.ds(start, chunk)] * scale


def split_pieces(pos, own, other, eig, snap_count, space_count):
    width, rows = own.shape
    chunk = rows // snap_count
    piece = jax.ShapeDtypeStruct((2, width, chunk), jnp.float32)
    return pl.pallas_call(
        lambda *refs: split_kernel(space_count, *refs),
        out_shape=[piece] * (snap_count // 2),
        in_specs=[IN_SMEM, IN_VMEM, IN_VMEM, IN_VMEM],
        out_specs=[IN_VMEM] * (snap_count // 2),
        compiler_params=params(4),
        name="split_pieces",
    )(pos, own, other, eig)


def stage_kernel(after_ref, source_ref, target_ref, sem):
    copy = pltpu.make_async_copy(source_ref, target_ref, sem)
    copy.start()
    copy.wait()


def stage(after, snapshots):
    size = snapshots.size * snapshots.dtype.itemsize
    return pl.pallas_call(
        stage_kernel,
        out_shape=jax.ShapeDtypeStruct(snapshots.shape, snapshots.dtype),
        in_specs=[IN_VMEM, IN_HBM],
        out_specs=IN_VMEM,
        scratch_shapes=[pltpu.SemaphoreType.DMA],
        compiler_params=params(12),
        cost_estimate=pl.CostEstimate(flops=0, bytes_accessed=2 * size, transcendentals=0),
        name="stage",
    )(after, snapshots)


def interleave(blocks):
    lane = lax.broadcasted_iota(jnp.int32, blocks[0].shape, 1) // ROW_BLOCK
    step = 1
    while step < GROUPS:
        high = (lane & step) != 0
        mixed = list(blocks)
        for a in range(GROUPS):
            if a & step == 0:
                b = a | step
                low_of_b = pltpu.roll(blocks[b], step * ROW_BLOCK, 1)
                high_of_a = pltpu.roll(blocks[a], LANES - step * ROW_BLOCK, 1)
                mixed[a] = jnp.where(high, low_of_b, blocks[a])
                mixed[b] = jnp.where(high, blocks[b], high_of_a)
        blocks = mixed
        step *= 2
    return blocks


def all_modes(slab_ref, q, slot, t):
    space_count, _, width, _ = slab_ref.shape
    low = lax.broadcasted_iota(jnp.int32, (SUBLANES, LANES), 0) < COL_BLOCK
    pairs = space_count // 2
    tiles = [None] * (space_count * width // SUBLANES)
    lanes = slice(t * LANES, (t + 1) * LANES)
    for u in range(pairs):
        for i in range(width // SUBLANES):
            rows = slice(i * SUBLANES, (i + 1) * SUBLANES)
            even = slab_ref[q ^ (2 * u), slot, rows, lanes]
            odd = slab_ref[q ^ (2 * u + 1), slot, rows, lanes]
            tiles[2 * i * pairs + u] = jnp.where(low, even, pltpu.roll(odd, COL_BLOCK, 0))
            tiles[(2 * i + 1) * pairs + u] = jnp.where(low, pltpu.roll(even, COL_BLOCK, 0), odd)
    return jnp.concatenate(tiles)


def multiply_kernel(pos_ref, slab_ref, snap_ref, out_ref, scaled_ref, cells_ref):
    p, q = pos_ref[0], pos_ref[1]
    _, snap_count, _, chunk = slab_ref.shape
    outer_count = snap_count // GROUPS
    for outer in range(outer_count):
        for t in range(chunk // LANES):
            slots = [p ^ (outer * GROUPS + g) for g in range(GROUPS)]
            for j, block in enumerate(interleave([all_modes(slab_ref, q, slot, t) for slot in slots])):
                tile = (t * GROUPS + j) * outer_count + outer
                scaled_ref[:, tile * LANES : (tile + 1) * LANES] = block.astype(jnp.bfloat16)
    total = lax.dot_general(
        snap_ref[...], scaled_ref[...], (((1,), (1,)), ((), ())), preferred_element_type=jnp.float32
    ).T
    cells = cells_ref.shape[2]
    for owner in range(snap_count):
        cells_ref[owner] = total[:, owner * cells : (owner + 1) * cells]
    for s in range(snap_count):
        out_ref[s] = cells_ref[p ^ s]


def multiply(pos, slab, snapshots):
    space_count, snap_count, width, _ = slab.shape
    cells, depth = snapshots.shape
    modes = width * space_count
    out = (snap_count, modes, cells // snap_count)
    return pl.pallas_call(
        multiply_kernel,
        out_shape=jax.ShapeDtypeStruct(out, jnp.float32),
        in_specs=[IN_SMEM, IN_VMEM, IN_VMEM],
        out_specs=IN_VMEM,
        scratch_shapes=[pltpu.VMEM((modes, depth), jnp.bfloat16), pltpu.VMEM(out, jnp.float32)],
        compiler_params=params(12),
        name="multiply",
    )(pos, slab, snapshots)


def pair_kernel(mine_ref, theirs_ref, *refs):
    held_refs, (coef_ref, *sum_refs) = refs[: len(refs) // 2], refs[len(refs) // 2 :]
    snap_count, modes, _ = mine_ref.shape
    total = jnp.zeros(coef_ref.shape, jnp.float32)
    sums = [mine_ref[s] + theirs_ref[s ^ 1] for s in range(snap_count)]
    for d, sum_ref in enumerate(sum_refs):
        sum_ref[...] = sums[2 * d]
    held = [held_refs[s // 2][s % 2].astype(jnp.bfloat16) for s in range(snap_count)]
    wide = jnp.concatenate(sums, axis=1)
    high = wide.astype(jnp.bfloat16)
    low = (wide - high.astype(jnp.float32)).astype(jnp.bfloat16)
    both = jnp.dot(
        jnp.concatenate([high, low]), jnp.concatenate(held), preferred_element_type=jnp.float32
    )
    coef_ref[...] = both[:modes] + both[modes:]


def pair(mine, theirs, held):
    snap_count, modes, cells = mine.shape
    columns = held[0].shape[2]
    return pl.pallas_call(
        pair_kernel,
        out_shape=[jax.ShapeDtypeStruct((modes, columns), jnp.float32)]
        + [jax.ShapeDtypeStruct((modes, cells), jnp.float32)] * (snap_count // 2),
        in_specs=[IN_VMEM] * (2 + len(held)),
        out_specs=[IN_VMEM] * (1 + snap_count // 2),
        compiler_params=params(6),
        name="pair",
    )(mine, theirs, *held)


def per_device(snapshots, vectors_cyclic, eigen_values, held_out):
    snap_count = lax.axis_size("snap")
    space_count = lax.axis_size("space")
    p, q = lax.axis_index("snap"), lax.axis_index("space")
    pos = jnp.stack([p, q]).astype(jnp.int32)
    chips = range(1, snap_count // 2)

    own = vectors_cyclic.T
    other = swap(own, "snap", 1)
    held_keep, held_send = widen(pos, held_out)
    held = jnp.stack([held_keep, swap(held_send, "snap", 1)])

    pieces = split_pieces(pos, own, other, eigen_values[None, :], snap_count, space_count)
    near = jnp.concatenate([pieces[0]] + [swap(pieces[d], "snap", 2 * d) for d in chips])
    near, held = lax.optimization_barrier((near, held))
    slab = jnp.stack([near] + [swap(near, "space", e) for e in range(1, space_count)])
    held = [held] + [swap(held, "snap", 2 * d) for d in chips]

    mine = multiply(pos, slab, stage(near, snapshots))
    coef, *sums = pair(mine, swap(mine, "snap", 1), held)

    coef = tree_sum([coef] + [swap(coef, "snap", 2 * d) for d in chips])
    coef = tree_sum([coef] + [swap(coef, "space", e) for e in range(1, space_count)])
    far = swap(coef, "snap", 1)
    first = p % 2 == 0
    coefficients = jnp.concatenate([jnp.where(first, coef, far), jnp.where(first, far, coef)], axis=1)

    modes = tree_sum([sums[0]] + [swap(sums[d], "snap", 2 * d) for d in chips])
    total_cells = snapshots.shape[0] * space_count
    return (modes.astype(jnp.bfloat16).T, coefficients / math.sqrt(total_cells))


def solution(mesh):
    return jax.shard_map(
        per_device,
        mesh=mesh,
        in_specs=(P("space", "snap"), P("snap", "space"), P(), P(("space", "snap"), None)),
        out_specs=(P(("space", "snap"), None), P()),
        check_vma=False,
    )
```

```python
import math

import jax
import jax.numpy as jnp
from jax import lax
from jax.experimental import pallas as pl
from jax.experimental.pallas import tpu as pltpu
from jax.sharding import PartitionSpec as P


ROW_BLOCK = 16
COL_BLOCK = 4
LANES = 128
SUBLANES = 8
GROUPS = LANES // ROW_BLOCK
MIB = 1 << 20
IN_SMEM = pl.BlockSpec(memory_space=pltpu.SMEM)
IN_VMEM = pl.BlockSpec(memory_space=pltpu.VMEM)
IN_HBM = pl.BlockSpec(memory_space=pltpu.HBM)


def params(mib):
    return pltpu.CompilerParams(vmem_limit_bytes=mib * MIB)


def swap(value, axis, mask):
    count = lax.axis_size(axis)
    return lax.ppermute(value, axis, [(i, i ^ mask) for i in range(count)])


def tree_sum(terms):
    while len(terms) > 1:
        terms = [terms[i] + terms[i + 1] for i in range(0, len(terms), 2)]
    return terms[0]


def prepare_kernel(space_count, pos_ref, own_ref, eig_ref, held_ref, scale_ref, keep_ref, send_ref, *own_refs):
    p, q = pos_ref[0], pos_ref[1]
    half = keep_ref.shape[1]
    core = p & 1
    keep_ref[...] = held_ref[:, pl.ds(pl.multiple_of(core * half, LANES), half)].astype(jnp.float32)
    send_ref[...] = held_ref[:, pl.ds(pl.multiple_of((1 - core) * half, LANES), half)].astype(jnp.float32)
    width = own_ref.shape[0]
    row = lax.broadcasted_iota(jnp.int32, (width, eig_ref.shape[1]), 0)
    mode = lax.broadcasted_iota(jnp.int32, (width, eig_ref.shape[1]), 1)
    mine = (row // COL_BLOCK * space_count + q) * COL_BLOCK + row % COL_BLOCK
    picked = jnp.where(mode == mine, eig_ref[...], 0.0)
    scale = lax.rsqrt(jnp.sum(picked, axis=1, keepdims=True))
    scale_ref[...] = jnp.broadcast_to(scale, scale_ref.shape)
    for d, out_ref in enumerate(own_refs):
        chunk = out_ref.shape[1]
        start = pl.multiple_of((p ^ (2 * d)) * chunk, LANES)
        out_ref[...] = own_ref[:, pl.ds(start, chunk)] * scale


def prepare(pos, own, eig, held, snap_count, space_count):
    width, rows = own.shape
    half = jax.ShapeDtypeStruct((held.shape[0], held.shape[1] // 2), jnp.float32)
    scale = jax.ShapeDtypeStruct((width, LANES), jnp.float32)
    piece = jax.ShapeDtypeStruct((width, rows // snap_count), jnp.float32)
    shapes = [scale, half, half] + [piece] * (snap_count // 2)
    return pl.pallas_call(
        lambda *refs: prepare_kernel(space_count, *refs),
        out_shape=shapes,
        in_specs=[IN_SMEM, IN_VMEM, IN_VMEM, IN_VMEM],
        out_specs=[IN_VMEM] * len(shapes),
        compiler_params=params(4),
        name="prepare",
    )(pos, own, eig, held)


def join_kernel(pos_ref, scale_ref, other_ref, *refs):
    p = pos_ref[0]
    own_refs, out_refs = refs[: len(refs) // 2], refs[len(refs) // 2 :]
    scale = scale_ref[:, :1]
    for d, (own_ref, out_ref) in enumerate(zip(own_refs, out_refs)):
        chunk = own_ref.shape[1]
        start = pl.multiple_of((p ^ (2 * d)) * chunk, LANES)
        out_ref[0] = own_ref[...]
        out_ref[1] = other_ref[:, pl.ds(start, chunk)] * scale


def join(pos, scale, other, own_pieces):
    piece = jax.ShapeDtypeStruct((2, *own_pieces[0].shape), jnp.float32)
    return pl.pallas_call(
        join_kernel,
        out_shape=[piece] * len(own_pieces),
        in_specs=[IN_SMEM] + [IN_VMEM] * (2 + len(own_pieces)),
        out_specs=[IN_VMEM] * len(own_pieces),
        compiler_params=params(4),
        name="join",
    )(pos, scale, other, *own_pieces)


def stage_kernel(after_ref, source_ref, target_ref, sem):
    copy = pltpu.make_async_copy(source_ref, target_ref, sem)
    copy.start()
    copy.wait()


def stage(after, snapshots):
    size = snapshots.size * snapshots.dtype.itemsize
    return pl.pallas_call(
        stage_kernel,
        out_shape=jax.ShapeDtypeStruct(snapshots.shape, snapshots.dtype),
        in_specs=[IN_VMEM, IN_HBM],
        out_specs=IN_VMEM,
        scratch_shapes=[pltpu.SemaphoreType.DMA],
        compiler_params=params(12),
        cost_estimate=pl.CostEstimate(flops=0, bytes_accessed=2 * size, transcendentals=0),
        name="stage",
    )(after, snapshots)


def interleave(blocks):
    lane = lax.broadcasted_iota(jnp.int32, blocks[0].shape, 1) // ROW_BLOCK
    step = 1
    while step < GROUPS:
        high = (lane & step) != 0
        mixed = list(blocks)
        for a in range(GROUPS):
            if a & step == 0:
                b = a | step
                low_of_b = pltpu.roll(blocks[b], step * ROW_BLOCK, 1)
                high_of_a = pltpu.roll(blocks[a], LANES - step * ROW_BLOCK, 1)
                mixed[a] = jnp.where(high, low_of_b, blocks[a])
                mixed[b] = jnp.where(high, blocks[b], high_of_a)
        blocks = mixed
        step *= 2
    return blocks


def all_modes(slab_ref, q, slot, t):
    space_count, _, width, _ = slab_ref.shape
    low = lax.broadcasted_iota(jnp.int32, (SUBLANES, LANES), 0) < COL_BLOCK
    pairs = space_count // 2
    tiles = [None] * (space_count * width // SUBLANES)
    lanes = slice(t * LANES, (t + 1) * LANES)
    for u in range(pairs):
        for i in range(width // SUBLANES):
            rows = slice(i * SUBLANES, (i + 1) * SUBLANES)
            even = slab_ref[q ^ (2 * u), slot, rows, lanes]
            odd = slab_ref[q ^ (2 * u + 1), slot, rows, lanes]
            tiles[2 * i * pairs + u] = jnp.where(low, even, pltpu.roll(odd, COL_BLOCK, 0))
            tiles[(2 * i + 1) * pairs + u] = jnp.where(low, pltpu.roll(even, COL_BLOCK, 0), odd)
    return jnp.concatenate(tiles)


def multiply_kernel(pos_ref, slab_ref, snap_ref, out_ref, scaled_ref, cells_ref):
    p, q = pos_ref[0], pos_ref[1]
    _, snap_count, _, chunk = slab_ref.shape
    outer_count = snap_count // GROUPS
    for outer in range(outer_count):
        for t in range(chunk // LANES):
            slots = [p ^ (outer * GROUPS + g) for g in range(GROUPS)]
            for j, block in enumerate(interleave([all_modes(slab_ref, q, slot, t) for slot in slots])):
                tile = (t * GROUPS + j) * outer_count + outer
                scaled_ref[:, tile * LANES : (tile + 1) * LANES] = block.astype(jnp.bfloat16)
    total = lax.dot_general(
        snap_ref[...], scaled_ref[...], (((1,), (1,)), ((), ())), preferred_element_type=jnp.float32
    ).T
    cells = cells_ref.shape[2]
    for owner in range(snap_count):
        cells_ref[owner] = total[:, owner * cells : (owner + 1) * cells]
    for s in range(snap_count):
        out_ref[s] = cells_ref[p ^ s]


def multiply(pos, slab, snapshots):
    space_count, snap_count, width, _ = slab.shape
    cells, depth = snapshots.shape
    modes = width * space_count
    out = (snap_count, modes, cells // snap_count)
    return pl.pallas_call(
        multiply_kernel,
        out_shape=jax.ShapeDtypeStruct(out, jnp.float32),
        in_specs=[IN_SMEM, IN_VMEM, IN_VMEM],
        out_specs=IN_VMEM,
        scratch_shapes=[pltpu.VMEM((modes, depth), jnp.bfloat16), pltpu.VMEM(out, jnp.float32)],
        compiler_params=params(12),
        name="multiply",
    )(pos, slab, snapshots)


def pair_kernel(mine_ref, theirs_ref, *refs):
    held_refs, (coef_ref, *sum_refs) = refs[: len(refs) // 2], refs[len(refs) // 2 :]
    snap_count, modes, _ = mine_ref.shape
    total = jnp.zeros(coef_ref.shape, jnp.float32)
    sums = [mine_ref[s] + theirs_ref[s ^ 1] for s in range(snap_count)]
    for d, sum_ref in enumerate(sum_refs):
        sum_ref[...] = sums[2 * d]
    held = [held_refs[s // 2][s % 2].astype(jnp.bfloat16) for s in range(snap_count)]
    wide = jnp.concatenate(sums, axis=1)
    high = wide.astype(jnp.bfloat16)
    low = (wide - high.astype(jnp.float32)).astype(jnp.bfloat16)
    both = jnp.dot(
        jnp.concatenate([high, low]), jnp.concatenate(held), preferred_element_type=jnp.float32
    )
    coef_ref[...] = both[:modes] + both[modes:]


def pair(mine, theirs, held):
    snap_count, modes, cells = mine.shape
    columns = held[0].shape[2]
    return pl.pallas_call(
        pair_kernel,
        out_shape=[jax.ShapeDtypeStruct((modes, columns), jnp.float32)]
        + [jax.ShapeDtypeStruct((modes, cells), jnp.float32)] * (snap_count // 2),
        in_specs=[IN_VMEM] * (2 + len(held)),
        out_specs=[IN_VMEM] * (1 + snap_count // 2),
        compiler_params=params(6),
        name="pair",
    )(mine, theirs, *held)


def per_device(snapshots, vectors_cyclic, eigen_values, held_out):
    snap_count = lax.axis_size("snap")
    space_count = lax.axis_size("space")
    p, q = lax.axis_index("snap"), lax.axis_index("space")
    pos = jnp.stack([p, q]).astype(jnp.int32)
    chips = range(1, snap_count // 2)
    others = range(1, space_count)

    own = vectors_cyclic.T
    other = swap(own, "snap", 1)
    scale, held_keep, held_send, *pieces = prepare(
        pos, own, eigen_values[None, :], held_out, snap_count, space_count
    )
    held = jnp.stack([held_keep, swap(held_send, "snap", 1)])
    pieces = join(pos, scale, other, pieces)
    near = jnp.concatenate([pieces[0]] + [swap(pieces[d], "snap", 2 * d) for d in chips])
    near, held = lax.optimization_barrier((near, held))
    slab = jnp.stack([near] + [swap(near, "space", e) for e in others])
    held = [held] + [swap(held, "snap", 2 * d) for d in chips]

    mine = multiply(pos, slab, stage(near, snapshots))
    coef, *sums = pair(mine, swap(mine, "snap", 1), held)

    coef = tree_sum([coef] + [swap(coef, "snap", 2 * d) for d in chips])
    coef = tree_sum([coef] + [swap(coef, "space", e) for e in others])
    far = swap(coef, "snap", 1)
    first = p % 2 == 0
    coefficients = jnp.concatenate([jnp.where(first, coef, far), jnp.where(first, far, coef)], axis=1)

    modes = tree_sum([sums[0]] + [swap(sums[d], "snap", 2 * d) for d in chips])
    total_cells = snapshots.shape[0] * space_count
    return (modes.astype(jnp.bfloat16).T, coefficients / math.sqrt(total_cells))


def solution(mesh):
    return jax.shard_map(
        per_device,
        mesh=mesh,
        in_specs=(P("space", "snap"), P("snap", "space"), P(), P(("space", "snap"), None)),
        out_specs=(P(("space", "snap"), None), P()),
        check_vma=False,
    )
```

```python
import math

import jax
import jax.numpy as jnp
from jax import lax
from jax.experimental import pallas as pl
from jax.experimental.pallas import tpu as pltpu
from jax.sharding import PartitionSpec as P


ROW_BLOCK = 16
COL_BLOCK = 4
LANES = 128
SUBLANES = 8
GROUPS = LANES // ROW_BLOCK
MIB = 1 << 20
IN_SMEM = pl.BlockSpec(memory_space=pltpu.SMEM)
IN_VMEM = pl.BlockSpec(memory_space=pltpu.VMEM)
IN_HBM = pl.BlockSpec(memory_space=pltpu.HBM)


def params(mib):
    return pltpu.CompilerParams(vmem_limit_bytes=mib * MIB)


def swap(value, axis, mask):
    count = lax.axis_size(axis)
    return lax.ppermute(value, axis, [(i, i ^ mask) for i in range(count)])


def tree_sum(terms):
    while len(terms) > 1:
        terms = [terms[i] + terms[i + 1] for i in range(0, len(terms), 2)]
    return terms[0]


def cut_kernel(pos_ref, source_ref, *out_refs):
    p = pos_ref[0]
    for d, out_ref in enumerate(out_refs):
        chunk = out_ref.shape[1]
        out_ref[...] = source_ref[:, pl.ds(pl.multiple_of((p ^ (2 * d)) * chunk, LANES), chunk)]


def cut(pos, source, snap_count):
    width, rows = source.shape
    piece = jax.ShapeDtypeStruct((width, rows // snap_count), jnp.float32)
    return pl.pallas_call(
        cut_kernel,
        out_shape=[piece] * (snap_count // 2),
        in_specs=[IN_SMEM, IN_VMEM],
        out_specs=[IN_VMEM] * (snap_count // 2),
        compiler_params=params(2),
        name="cut",
    )(pos, source)


def join_kernel(pos_ref, source_ref, *refs):
    p = pos_ref[0]
    own_refs, out_refs = refs[: len(refs) // 2], refs[len(refs) // 2 :]
    for d, (own_ref, out_ref) in enumerate(zip(own_refs, out_refs)):
        chunk = own_ref.shape[1]
        out_ref[0] = own_ref[...]
        out_ref[1] = source_ref[:, pl.ds(pl.multiple_of((p ^ (2 * d)) * chunk, LANES), chunk)]


def join(pos, source, own_pieces):
    piece = jax.ShapeDtypeStruct((2, *own_pieces[0].shape), jnp.float32)
    return pl.pallas_call(
        join_kernel,
        out_shape=[piece] * len(own_pieces),
        in_specs=[IN_SMEM] + [IN_VMEM] * (1 + len(own_pieces)),
        out_specs=[IN_VMEM] * len(own_pieces),
        compiler_params=params(2),
        name="join",
    )(pos, source, *own_pieces)


def stage_kernel(after_ref, source_ref, target_ref, sems):
    rows = source_ref.shape[0] // sems.shape[0]
    parts = [pl.ds(i * rows, rows) for i in range(sems.shape[0])]
    copies = [pltpu.make_async_copy(source_ref.at[r], target_ref.at[r], sems.at[i]) for i, r in enumerate(parts)]
    for copy in copies:
        copy.start()
    for copy in copies:
        copy.wait()


def stage(after, snapshots):
    return pl.pallas_call(
        stage_kernel,
        out_shape=jax.ShapeDtypeStruct(snapshots.shape, snapshots.dtype),
        in_specs=[IN_HBM, IN_HBM],
        out_specs=IN_VMEM,
        scratch_shapes=[pltpu.SemaphoreType.DMA((4,))],
        compiler_params=params(42),
        name="stage",
    )(after, snapshots)


def interleave(blocks):
    lane = lax.broadcasted_iota(jnp.int32, blocks[0].shape, 1) // ROW_BLOCK
    step = 1
    while step < GROUPS:
        high = (lane & step) != 0
        mixed = list(blocks)
        for a in range(GROUPS):
            if a & step == 0:
                b = a | step
                low_of_b = pltpu.roll(blocks[b], step * ROW_BLOCK, 1)
                high_of_a = pltpu.roll(blocks[a], LANES - step * ROW_BLOCK, 1)
                mixed[a] = jnp.where(high, low_of_b, blocks[a])
                mixed[b] = jnp.where(high, blocks[b], high_of_a)
        blocks = mixed
        step *= 2
    return blocks


def all_modes(slab_ref, q, slot, t):
    space_count, _, width, _ = slab_ref.shape
    low = lax.broadcasted_iota(jnp.int32, (SUBLANES, LANES), 0) < COL_BLOCK
    pairs = space_count // 2
    tiles = [None] * (space_count * width // SUBLANES)
    lanes = slice(t * LANES, (t + 1) * LANES)
    for u in range(pairs):
        for i in range(width // SUBLANES):
            rows = slice(i * SUBLANES, (i + 1) * SUBLANES)
            even = slab_ref[q ^ (2 * u), slot, rows, lanes]
            odd = slab_ref[q ^ (2 * u + 1), slot, rows, lanes]
            tiles[2 * i * pairs + u] = jnp.where(low, even, pltpu.roll(odd, COL_BLOCK, 0))
            tiles[(2 * i + 1) * pairs + u] = jnp.where(low, pltpu.roll(even, COL_BLOCK, 0), odd)
    return jnp.concatenate(tiles)


def scale_column(eig):
    modes = eig.shape[1]
    row = lax.broadcasted_iota(jnp.int32, (modes, modes), 0)
    column = lax.broadcasted_iota(jnp.int32, (modes, modes), 1)
    value = jnp.sum(jnp.where(row == column, eig, 0.0), axis=1, keepdims=True)
    return jnp.broadcast_to(lax.rsqrt(value), (modes, LANES))


def multiply_kernel(pos_ref, eig_ref, slab_ref, snap_ref, out_ref, scaled_ref, cells_ref):
    p, q = pos_ref[0], pos_ref[1]
    _, snap_count, _, chunk = slab_ref.shape
    outer_count = snap_count // GROUPS
    scale = scale_column(eig_ref[...])
    for outer in range(outer_count):
        for t in range(chunk // LANES):
            slots = [p ^ (outer * GROUPS + g) for g in range(GROUPS)]
            for j, block in enumerate(interleave([all_modes(slab_ref, q, slot, t) for slot in slots])):
                tile = (t * GROUPS + j) * outer_count + outer
                scaled_ref[:, tile * LANES : (tile + 1) * LANES] = (block * scale).astype(jnp.bfloat16)
    total = lax.dot_general(
        snap_ref[...], scaled_ref[...], (((1,), (1,)), ((), ())), preferred_element_type=jnp.float32
    ).T
    cells = cells_ref.shape[2]
    for owner in range(snap_count):
        cells_ref[owner] = total[:, owner * cells : (owner + 1) * cells]
    for s in range(snap_count):
        out_ref[s] = cells_ref[p ^ s]


def multiply(pos, eig, slab, snapshots):
    space_count, snap_count, width, _ = slab.shape
    cells, depth = snapshots.shape
    modes = width * space_count
    out = (snap_count, modes, cells // snap_count)
    return pl.pallas_call(
        multiply_kernel,
        out_shape=jax.ShapeDtypeStruct(out, jnp.float32),
        in_specs=[IN_SMEM, IN_VMEM, IN_VMEM, IN_VMEM],
        out_specs=IN_VMEM,
        scratch_shapes=[pltpu.VMEM((modes, depth), jnp.bfloat16), pltpu.VMEM(out, jnp.float32)],
        compiler_params=params(12),
        name="multiply",
    )(pos, eig, slab, snapshots)


def pair_kernel(mine_ref, theirs_ref, *refs):
    held_refs, out_refs = refs[: len(refs) // 2], refs[len(refs) // 2 :]
    snap_count, modes, _ = mine_ref.shape
    sums = [mine_ref[s] + theirs_ref[s ^ 1] for s in range(snap_count)]
    held = [held_refs[s // 2][s % 2].astype(jnp.bfloat16) for s in range(snap_count)]
    wide = jnp.concatenate(sums, axis=1)
    high = wide.astype(jnp.bfloat16)
    low = (wide - high.astype(jnp.float32)).astype(jnp.bfloat16)
    both = jnp.dot(jnp.concatenate([high, low]), jnp.concatenate(held), preferred_element_type=jnp.float32)
    coef = both[:modes] + both[modes:]
    for d, out_ref in enumerate(out_refs):
        out_ref[:, : coef.shape[1]] = coef
        out_ref[:, coef.shape[1] :] = sums[2 * d]


def pair(mine, theirs, held):
    snap_count, modes, cells = mine.shape
    out = jax.ShapeDtypeStruct((modes, held[0].shape[2] + cells), jnp.float32)
    return pl.pallas_call(
        pair_kernel,
        out_shape=[out] * (snap_count // 2),
        in_specs=[IN_VMEM] * (2 + len(held)),
        out_specs=[IN_VMEM] * (snap_count // 2),
        compiler_params=params(6),
        name="pair",
    )(mine, theirs, *held)


def per_device(snapshots, vectors_cyclic, eigen_values, held_out):
    snap_count = lax.axis_size("snap")
    space_count = lax.axis_size("space")
    p, q = lax.axis_index("snap"), lax.axis_index("space")
    pos = jnp.stack([p, q]).astype(jnp.int32)
    chips = range(1, snap_count // 2)
    others = range(1, space_count)

    own = vectors_cyclic.T
    other = swap(own, "snap", 1)
    pieces = join(pos, other, cut(pos, own, snap_count))
    near = [pieces[0]] + [swap(pieces[d], "snap", 2 * d) for d in chips]

    first, second = near[0], jnp.concatenate(near[1:])
    firsts = [first] + [swap(first, "space", e) for e in others]
    seconds = [second] + [swap(second, "space", e) for e in others]
    slab = jnp.stack([jnp.concatenate(parts) for parts in zip(firsts, seconds)])

    half = held_out.shape[1] // 2
    wide = held_out.astype(jnp.float32)
    held_keep = lax.dynamic_slice_in_dim(wide, (p & 1) * half, half, 1)
    held_send = lax.dynamic_slice_in_dim(wide, (1 - (p & 1)) * half, half, 1)
    held = jnp.stack([held_keep, swap(held_send, "snap", 1)])
    held = [held] + [swap(held, "snap", 2 * d) for d in chips]

    mine = multiply(pos, eigen_values[None, :], slab, stage(pieces[0], snapshots))
    both = pair(mine, swap(mine, "snap", 1), held)
    both = tree_sum([both[0]] + [swap(both[d], "snap", 2 * d) for d in chips])
    coef, modes = both[:, :half], both[:, half:]
    coef = tree_sum([coef] + [swap(coef, "space", e) for e in others])
    far = swap(coef, "snap", 1)
    even = p % 2 == 0
    coefficients = jnp.concatenate([jnp.where(even, coef, far), jnp.where(even, far, coef)], axis=1)

    total_cells = snapshots.shape[0] * space_count
    return (modes.astype(jnp.bfloat16).T, coefficients / math.sqrt(total_cells))


def solution(mesh):
    return jax.shard_map(
        per_device,
        mesh=mesh,
        in_specs=(P("space", "snap"), P("snap", "space"), P(), P(("space", "snap"), None)),
        out_specs=(P(("space", "snap"), None), P()),
        check_vma=False,
    )
```

```python
import math

import jax
import jax.numpy as jnp
from jax import lax
from jax.experimental import pallas as pl
from jax.experimental.pallas import tpu as pltpu
from jax.sharding import PartitionSpec as P


ROW_BLOCK = 16
COL_BLOCK = 4
LANES = 128
SUBLANES = 8
GROUPS = LANES // ROW_BLOCK
MIB = 1 << 20
LONG = pl.CostEstimate(flops=20_000_000_000, bytes_accessed=1000, transcendentals=0)
IN_VMEM = pl.BlockSpec(memory_space=pltpu.VMEM)


def params(mib):
    return pltpu.CompilerParams(vmem_limit_bytes=mib * MIB)


def swap(value, axis, mask):
    count = lax.axis_size(axis)
    return lax.ppermute(value, axis, [(i, i ^ mask) for i in range(count)])


def tree_sum(terms):
    while len(terms) > 1:
        terms = [terms[i] + terms[i + 1] for i in range(0, len(terms), 2)]
    return terms[0]


def cut_kernel(source_ref, *out_refs):
    p = lax.axis_index("snap")
    for d, out_ref in enumerate(out_refs):
        chunk = out_ref.shape[1]
        out_ref[...] = source_ref[:, pl.ds(pl.multiple_of((p ^ (2 * d)) * chunk, LANES), chunk)]


def cut(source, snap_count):
    width, rows = source.shape
    piece = jax.ShapeDtypeStruct((width, rows // snap_count), jnp.float32)
    return pl.pallas_call(
        cut_kernel,
        out_shape=[piece] * (snap_count // 2),
        in_specs=[IN_VMEM],
        out_specs=[IN_VMEM] * (snap_count // 2),
        compiler_params=params(2),
        cost_estimate=LONG,
        name="cut",
    )(source)


def join_kernel(source_ref, *refs):
    p = lax.axis_index("snap")
    own_refs, out_refs = refs[: len(refs) // 2], refs[len(refs) // 2 :]
    for d, (own_ref, out_ref) in enumerate(zip(own_refs, out_refs)):
        chunk = own_ref.shape[1]
        out_ref[0] = own_ref[...]
        out_ref[1] = source_ref[:, pl.ds(pl.multiple_of((p ^ (2 * d)) * chunk, LANES), chunk)]


def join(source, own_pieces):
    piece = jax.ShapeDtypeStruct((2, *own_pieces[0].shape), jnp.float32)
    return pl.pallas_call(
        join_kernel,
        out_shape=[piece] * len(own_pieces),
        in_specs=[IN_VMEM] * (1 + len(own_pieces)),
        out_specs=[IN_VMEM] * len(own_pieces),
        compiler_params=params(2),
        cost_estimate=LONG,
        name="join",
    )(source, *own_pieces)


def interleave(blocks):
    lane = lax.broadcasted_iota(jnp.int32, blocks[0].shape, 1) // ROW_BLOCK
    step = 1
    while step < GROUPS:
        high = (lane & step) != 0
        mixed = list(blocks)
        for a in range(GROUPS):
            if a & step == 0:
                b = a | step
                low_of_b = pltpu.roll(blocks[b], step * ROW_BLOCK, 1)
                high_of_a = pltpu.roll(blocks[a], LANES - step * ROW_BLOCK, 1)
                mixed[a] = jnp.where(high, low_of_b, blocks[a])
                mixed[b] = jnp.where(high, blocks[b], high_of_a)
        blocks = mixed
        step *= 2
    return blocks


def all_modes(slab_ref, q, slot, t):
    space_count, _, width, _ = slab_ref.shape
    low = lax.broadcasted_iota(jnp.int32, (SUBLANES, LANES), 0) < COL_BLOCK
    pairs = space_count // 2
    tiles = [None] * (space_count * width // SUBLANES)
    lanes = slice(t * LANES, (t + 1) * LANES)
    for u in range(pairs):
        for i in range(width // SUBLANES):
            rows = slice(i * SUBLANES, (i + 1) * SUBLANES)
            even = slab_ref[q ^ (2 * u), slot, rows, lanes]
            odd = slab_ref[q ^ (2 * u + 1), slot, rows, lanes]
            tiles[2 * i * pairs + u] = jnp.where(low, even, pltpu.roll(odd, COL_BLOCK, 0))
            tiles[(2 * i + 1) * pairs + u] = jnp.where(low, pltpu.roll(even, COL_BLOCK, 0), odd)
    return jnp.concatenate(tiles)


def scale_column(eig):
    modes = eig.shape[1]
    row = lax.broadcasted_iota(jnp.int32, (modes, modes), 0)
    column = lax.broadcasted_iota(jnp.int32, (modes, modes), 1)
    value = jnp.sum(jnp.where(row == column, eig, 0.0), axis=1, keepdims=True)
    return jnp.broadcast_to(lax.rsqrt(value), (modes, LANES))


def multiply_kernel(eig_ref, slab_ref, snap_ref, out_ref, scaled_ref, cells_ref):
    p, q = lax.axis_index("snap"), lax.axis_index("space")
    _, snap_count, _, chunk = slab_ref.shape
    outer_count = snap_count // GROUPS
    scale = scale_column(eig_ref[...])
    for outer in range(outer_count):
        for t in range(chunk // LANES):
            slots = [p ^ (outer * GROUPS + g) for g in range(GROUPS)]
            for j, block in enumerate(interleave([all_modes(slab_ref, q, slot, t) for slot in slots])):
                tile = (t * GROUPS + j) * outer_count + outer
                scaled_ref[:, tile * LANES : (tile + 1) * LANES] = (block * scale).astype(jnp.bfloat16)
    total = lax.dot_general(
        snap_ref[...], scaled_ref[...], (((1,), (1,)), ((), ())), preferred_element_type=jnp.float32
    ).T
    cells = cells_ref.shape[2]
    for owner in range(snap_count):
        cells_ref[owner] = total[:, owner * cells : (owner + 1) * cells]
    for s in range(snap_count):
        out_ref[s] = cells_ref[p ^ s]


def multiply(eig, slab, snapshots):
    space_count, snap_count, width, _ = slab.shape
    cells, depth = snapshots.shape
    modes = width * space_count
    out = (snap_count, modes, cells // snap_count)
    return pl.pallas_call(
        multiply_kernel,
        out_shape=jax.ShapeDtypeStruct(out, jnp.float32),
        in_specs=[IN_VMEM] * 3,
        out_specs=IN_VMEM,
        scratch_shapes=[pltpu.VMEM((modes, depth), jnp.bfloat16), pltpu.VMEM(out, jnp.float32)],
        compiler_params=params(12),
        name="multiply",
    )(eig, slab, snapshots)


def pair_kernel(mine_ref, theirs_ref, *refs):
    held_refs, out_refs = refs[: len(refs) // 2], refs[len(refs) // 2 :]
    snap_count, modes, _ = mine_ref.shape
    sums = [mine_ref[s] + theirs_ref[s ^ 1] for s in range(snap_count)]
    held = [held_refs[s // 2][s % 2].astype(jnp.bfloat16) for s in range(snap_count)]
    wide = jnp.concatenate(sums, axis=1)
    high = wide.astype(jnp.bfloat16)
    low = (wide - high.astype(jnp.float32)).astype(jnp.bfloat16)
    both = jnp.dot(jnp.concatenate([high, low]), jnp.concatenate(held), preferred_element_type=jnp.float32)
    coef = both[:modes] + both[modes:]
    for d, out_ref in enumerate(out_refs):
        out_ref[:, : coef.shape[1]] = coef
        out_ref[:, coef.shape[1] :] = sums[2 * d]


def pair(mine, theirs, held):
    snap_count, modes, cells = mine.shape
    out = jax.ShapeDtypeStruct((modes, held[0].shape[2] + cells), jnp.float32)
    return pl.pallas_call(
        pair_kernel,
        out_shape=[out] * (snap_count // 2),
        in_specs=[IN_VMEM] * (2 + len(held)),
        out_specs=[IN_VMEM] * (snap_count // 2),
        compiler_params=params(6),
        name="pair",
    )(mine, theirs, *held)


def per_device(snapshots, vectors_cyclic, eigen_values, held_out):
    snap_count = lax.axis_size("snap")
    space_count = lax.axis_size("space")
    p = lax.axis_index("snap")
    chips = range(1, snap_count // 2)
    others = range(1, space_count)

    own = vectors_cyclic.T
    other = swap(own, "snap", 1)
    pieces = join(other, cut(own, snap_count))
    near = [pieces[0]] + [swap(pieces[d], "snap", 2 * d) for d in chips]

    first, second = jnp.concatenate(near[:2]), jnp.concatenate(near[2:])
    firsts = [first] + [swap(first, "space", e) for e in others]
    seconds = [second] + [swap(second, "space", e) for e in others]
    slab = jnp.stack([jnp.concatenate(parts) for parts in zip(firsts, seconds)])

    half = held_out.shape[1] // 2
    wide = held_out.astype(jnp.float32)
    held_keep = lax.dynamic_slice_in_dim(wide, (p & 1) * half, half, 1)
    held_send = lax.dynamic_slice_in_dim(wide, (1 - (p & 1)) * half, half, 1)
    held = jnp.stack([held_keep, swap(held_send, "snap", 1)])
    held = [held] + [swap(held, "snap", 2 * d) for d in chips]

    mine = multiply(eigen_values[None, :], slab, snapshots)
    both = pair(mine, swap(mine, "snap", 1), held)
    both = tree_sum([both[0]] + [swap(both[d], "snap", 2 * d) for d in chips])
    coef, modes = both[:, :half], both[:, half:]
    coef = tree_sum([coef] + [swap(coef, "space", e) for e in others])
    far = swap(coef, "snap", 1)
    even = p % 2 == 0
    coefficients = jnp.concatenate([jnp.where(even, coef, far), jnp.where(even, far, coef)], axis=1)

    total_cells = snapshots.shape[0] * space_count
    return (modes.astype(jnp.bfloat16).T, coefficients / math.sqrt(total_cells))


def solution(mesh):
    return jax.shard_map(
        per_device,
        mesh=mesh,
        in_specs=(P("space", "snap"), P("snap", "space"), P(), P(("space", "snap"), None)),
        out_specs=(P(("space", "snap"), None), P()),
        check_vma=False,
    )
```

```python
import math

import jax
import jax.numpy as jnp
from jax import lax
from jax.experimental import pallas as pl
from jax.experimental.pallas import tpu as pltpu
from jax.sharding import PartitionSpec as P


ROW_BLOCK = 16
COL_BLOCK = 4
LANES = 128
SUBLANES = 8
GROUPS = LANES // ROW_BLOCK
MIB = 1 << 20
LONG = pl.CostEstimate(flops=20_000_000_000, bytes_accessed=1000, transcendentals=0)
IN_VMEM = pl.BlockSpec(memory_space=pltpu.VMEM)


def params(mib):
    return pltpu.CompilerParams(vmem_limit_bytes=mib * MIB)


def swap(value, axis, mask):
    count = lax.axis_size(axis)
    return lax.ppermute(value, axis, [(i, i ^ mask) for i in range(count)])


def tree_sum(terms):
    while len(terms) > 1:
        terms = [terms[i] + terms[i + 1] for i in range(0, len(terms), 2)]
    return terms[0]


def cut_kernel(source_ref, *out_refs):
    p = lax.axis_index("snap")
    for d, out_ref in enumerate(out_refs):
        chunk = out_ref.shape[1]
        out_ref[...] = source_ref[:, pl.ds(pl.multiple_of((p ^ (2 * d)) * chunk, LANES), chunk)]


def cut(source, snap_count):
    width, rows = source.shape
    piece = jax.ShapeDtypeStruct((width, rows // snap_count), jnp.float32)
    return pl.pallas_call(
        cut_kernel,
        out_shape=[piece] * (snap_count // 2),
        in_specs=[IN_VMEM],
        out_specs=[IN_VMEM] * (snap_count // 2),
        compiler_params=params(2),
        cost_estimate=LONG,
        name="cut",
    )(source)


def join_kernel(source_ref, *refs):
    p = lax.axis_index("snap")
    own_refs, out_refs = refs[: len(refs) // 2], refs[len(refs) // 2 :]
    for d, (own_ref, out_ref) in enumerate(zip(own_refs, out_refs)):
        chunk = own_ref.shape[1]
        out_ref[0] = own_ref[...]
        out_ref[1] = source_ref[:, pl.ds(pl.multiple_of((p ^ (2 * d)) * chunk, LANES), chunk)]


def join(source, own_pieces):
    piece = jax.ShapeDtypeStruct((2, *own_pieces[0].shape), jnp.float32)
    return pl.pallas_call(
        join_kernel,
        out_shape=[piece] * len(own_pieces),
        in_specs=[IN_VMEM] * (1 + len(own_pieces)),
        out_specs=[IN_VMEM] * len(own_pieces),
        compiler_params=params(2),
        cost_estimate=LONG,
        name="join",
    )(source, *own_pieces)


def interleave(blocks):
    lane = lax.broadcasted_iota(jnp.int32, blocks[0].shape, 1) // ROW_BLOCK
    step = 1
    while step < GROUPS:
        high = (lane & step) != 0
        mixed = list(blocks)
        for a in range(GROUPS):
            if a & step == 0:
                b = a | step
                low_of_b = pltpu.roll(blocks[b], step * ROW_BLOCK, 1)
                high_of_a = pltpu.roll(blocks[a], LANES - step * ROW_BLOCK, 1)
                mixed[a] = jnp.where(high, low_of_b, blocks[a])
                mixed[b] = jnp.where(high, blocks[b], high_of_a)
        blocks = mixed
        step *= 2
    return blocks


def all_modes(slab_ref, q, slot, t):
    space_count, _, width, _ = slab_ref.shape
    low = lax.broadcasted_iota(jnp.int32, (SUBLANES, LANES), 0) < COL_BLOCK
    pairs = space_count // 2
    tiles = [None] * (space_count * width // SUBLANES)
    lanes = slice(t * LANES, (t + 1) * LANES)
    for u in range(pairs):
        for i in range(width // SUBLANES):
            rows = slice(i * SUBLANES, (i + 1) * SUBLANES)
            even = slab_ref[q ^ (2 * u), slot, rows, lanes]
            odd = slab_ref[q ^ (2 * u + 1), slot, rows, lanes]
            tiles[2 * i * pairs + u] = jnp.where(low, even, pltpu.roll(odd, COL_BLOCK, 0))
            tiles[(2 * i + 1) * pairs + u] = jnp.where(low, pltpu.roll(even, COL_BLOCK, 0), odd)
    return jnp.concatenate(tiles)


def scale_column(eig):
    modes = eig.shape[1]
    row = lax.broadcasted_iota(jnp.int32, (modes, modes), 0)
    column = lax.broadcasted_iota(jnp.int32, (modes, modes), 1)
    value = jnp.sum(jnp.where(row == column, eig, 0.0), axis=1, keepdims=True)
    return jnp.broadcast_to(lax.rsqrt(value), (modes, LANES))


def multiply_kernel(eig_ref, slab_ref, snap_ref, out_ref, scaled_ref, cells_ref):
    p, q = lax.axis_index("snap"), lax.axis_index("space")
    _, snap_count, _, chunk = slab_ref.shape
    outer_count = snap_count // GROUPS
    scale = scale_column(eig_ref[...])
    for outer in range(outer_count):
        for t in range(chunk // LANES):
            slots = [p ^ (outer * GROUPS + g) for g in range(GROUPS)]
            for j, block in enumerate(interleave([all_modes(slab_ref, q, slot, t) for slot in slots])):
                tile = (t * GROUPS + j) * outer_count + outer
                scaled_ref[:, tile * LANES : (tile + 1) * LANES] = (block * scale).astype(jnp.bfloat16)
    total = lax.dot_general(
        snap_ref[...], scaled_ref[...], (((1,), (1,)), ((), ())), preferred_element_type=jnp.float32
    ).T
    cells = cells_ref.shape[2]
    for owner in range(snap_count):
        cells_ref[owner] = total[:, owner * cells : (owner + 1) * cells]
    for s in range(snap_count):
        out_ref[s] = cells_ref[p ^ s]


def multiply(eig, slab, snapshots):
    space_count, snap_count, width, _ = slab.shape
    cells, depth = snapshots.shape
    modes = width * space_count
    out = (snap_count, modes, cells // snap_count)
    return pl.pallas_call(
        multiply_kernel,
        out_shape=jax.ShapeDtypeStruct(out, jnp.float32),
        in_specs=[IN_VMEM] * 3,
        out_specs=IN_VMEM,
        scratch_shapes=[pltpu.VMEM((modes, depth), jnp.bfloat16), pltpu.VMEM(out, jnp.float32)],
        compiler_params=params(12),
        name="multiply",
    )(eig, slab, snapshots)


def pair_kernel(count, mine_ref, theirs_ref, *refs):
    held_refs, (coef_ref, next_ref, *sum_refs) = refs[:count], refs[count:]
    snap_count, modes, _ = mine_ref.shape
    sums = [mine_ref[s] + theirs_ref[s ^ 1] for s in range(snap_count)]
    held = [held_refs[s // 2][s % 2].astype(jnp.bfloat16) for s in range(snap_count)]
    wide = jnp.concatenate(sums, axis=1)
    high = wide.astype(jnp.bfloat16)
    low = (wide - high.astype(jnp.float32)).astype(jnp.bfloat16)
    both = jnp.dot(jnp.concatenate([high, low]), jnp.concatenate(held), preferred_element_type=jnp.float32)
    coef = both[:modes] + both[modes:]
    coef_ref[...] = coef
    next_ref[:, : coef.shape[1]] = coef
    next_ref[:, coef.shape[1] :] = sums[2]
    for sum_ref, d in zip(sum_refs, [0, *range(2, count)]):
        sum_ref[...] = sums[2 * d]


def pair(mine, theirs, held):
    _, modes, cells = mine.shape
    columns = held[0].shape[2]
    shapes = [(modes, columns), (modes, columns + cells)] + [(modes, cells)] * (len(held) - 1)
    return pl.pallas_call(
        lambda *refs: pair_kernel(len(held), *refs),
        out_shape=[jax.ShapeDtypeStruct(shape, jnp.float32) for shape in shapes],
        in_specs=[IN_VMEM] * (2 + len(held)),
        out_specs=[IN_VMEM] * len(shapes),
        compiler_params=params(6),
        name="pair",
    )(mine, theirs, *held)


def per_device(snapshots, vectors_cyclic, eigen_values, held_out):
    snap_count = lax.axis_size("snap")
    space_count = lax.axis_size("space")
    p = lax.axis_index("snap")
    chips = range(1, snap_count // 2)
    others = range(1, space_count)

    own = vectors_cyclic.T
    other = swap(own, "snap", 1)
    pieces = join(other, cut(own, snap_count))
    near = [pieces[0]] + [swap(pieces[d], "snap", 2 * d) for d in chips]

    first, second = jnp.concatenate(near[:2]), jnp.concatenate(near[2:])
    firsts = [first] + [swap(first, "space", e) for e in others]
    seconds = [second] + [swap(second, "space", e) for e in others]
    slab = jnp.stack([jnp.concatenate(parts) for parts in zip(firsts, seconds)])

    half = held_out.shape[1] // 2
    wide = held_out.astype(jnp.float32)
    held_keep = lax.dynamic_slice_in_dim(wide, (p & 1) * half, half, 1)
    held_send = lax.dynamic_slice_in_dim(wide, (1 - (p & 1)) * half, half, 1)
    held = jnp.stack([held_keep, swap(held_send, "snap", 1)])
    held = [held] + [swap(held, "snap", 2 * d) for d in chips]

    mine = multiply(eigen_values[None, :], slab, snapshots)
    coef, beside, *sums = pair(mine, swap(mine, "snap", 1), held)
    beside = swap(beside, "snap", 2)
    coef = tree_sum([coef, beside[:, :half]] + [swap(coef, "snap", 2 * d) for d in chips[1:]])
    terms = [sums[0], beside[:, half:]] + [swap(sums[d - 1], "snap", 2 * d) for d in chips[1:]]
    coef = tree_sum([coef] + [swap(coef, "space", e) for e in others])
    modes = tree_sum(lax.optimization_barrier((terms, coef))[0])
    far = swap(coef, "snap", 1)
    even = p % 2 == 0
    coefficients = jnp.concatenate([jnp.where(even, coef, far), jnp.where(even, far, coef)], axis=1)

    total_cells = snapshots.shape[0] * space_count
    return (modes.astype(jnp.bfloat16).T, coefficients / math.sqrt(total_cells))


def solution(mesh):
    return jax.shard_map(
        per_device,
        mesh=mesh,
        in_specs=(P("space", "snap"), P("snap", "space"), P(), P(("space", "snap"), None)),
        out_specs=(P(("space", "snap"), None), P()),
        check_vma=False,
    )
```

```python
import math

import jax
import jax.numpy as jnp
from jax import lax
from jax.experimental import pallas as pl
from jax.experimental.pallas import tpu as pltpu
from jax.sharding import PartitionSpec as P


ROW_BLOCK = 16
COL_BLOCK = 4
LANES = 128
SUBLANES = 8
GROUPS = LANES // ROW_BLOCK
MIB = 1 << 20
LONG = pl.CostEstimate(flops=20_000_000_000, bytes_accessed=1000, transcendentals=0)
IN_VMEM = pl.BlockSpec(memory_space=pltpu.VMEM)


def params(mib):
    return pltpu.CompilerParams(vmem_limit_bytes=mib * MIB)


def swap(value, axis, mask):
    count = lax.axis_size(axis)
    return lax.ppermute(value, axis, [(i, i ^ mask) for i in range(count)])


def tree_sum(terms):
    while len(terms) > 1:
        terms = [terms[i] + terms[i + 1] for i in range(0, len(terms), 2)]
    return terms[0]


def cut_kernel(source_ref, *out_refs):
    p = lax.axis_index("snap")
    for d, out_ref in enumerate(out_refs):
        chunk = out_ref.shape[1]
        out_ref[...] = source_ref[:, pl.ds(pl.multiple_of((p ^ (2 * d)) * chunk, LANES), chunk)]


def cut(source, snap_count):
    width, rows = source.shape
    piece = jax.ShapeDtypeStruct((width, rows // snap_count), jnp.float32)
    return pl.pallas_call(
        cut_kernel,
        out_shape=[piece] * (snap_count // 2),
        in_specs=[IN_VMEM],
        out_specs=[IN_VMEM] * (snap_count // 2),
        compiler_params=params(2),
        cost_estimate=LONG,
        name="cut",
    )(source)


def join_kernel(source_ref, *refs):
    p = lax.axis_index("snap")
    own_refs, out_refs = refs[: len(refs) // 2], refs[len(refs) // 2 :]
    for d, (own_ref, out_ref) in enumerate(zip(own_refs, out_refs)):
        chunk = own_ref.shape[1]
        out_ref[0] = own_ref[...]
        out_ref[1] = source_ref[:, pl.ds(pl.multiple_of((p ^ (2 * d)) * chunk, LANES), chunk)]


def join(source, own_pieces):
    piece = jax.ShapeDtypeStruct((2, *own_pieces[0].shape), jnp.float32)
    return pl.pallas_call(
        join_kernel,
        out_shape=[piece] * len(own_pieces),
        in_specs=[IN_VMEM] * (1 + len(own_pieces)),
        out_specs=[IN_VMEM] * len(own_pieces),
        compiler_params=params(2),
        cost_estimate=LONG,
        name="join",
    )(source, *own_pieces)


def interleave(blocks):
    lane = lax.broadcasted_iota(jnp.int32, blocks[0].shape, 1) // ROW_BLOCK
    step = 1
    while step < GROUPS:
        high = (lane & step) != 0
        mixed = list(blocks)
        for a in range(GROUPS):
            if a & step == 0:
                b = a | step
                low_of_b = pltpu.roll(blocks[b], step * ROW_BLOCK, 1)
                high_of_a = pltpu.roll(blocks[a], LANES - step * ROW_BLOCK, 1)
                mixed[a] = jnp.where(high, low_of_b, blocks[a])
                mixed[b] = jnp.where(high, blocks[b], high_of_a)
        blocks = mixed
        step *= 2
    return blocks


def all_modes(slab_ref, q, slot, t):
    space_count, _, width, _ = slab_ref.shape
    low = lax.broadcasted_iota(jnp.int32, (SUBLANES, LANES), 0) < COL_BLOCK
    pairs = space_count // 2
    tiles = [None] * (space_count * width // SUBLANES)
    lanes = slice(t * LANES, (t + 1) * LANES)
    for u in range(pairs):
        for i in range(width // SUBLANES):
            rows = slice(i * SUBLANES, (i + 1) * SUBLANES)
            even = slab_ref[q ^ (2 * u), slot, rows, lanes]
            odd = slab_ref[q ^ (2 * u + 1), slot, rows, lanes]
            tiles[2 * i * pairs + u] = jnp.where(low, even, pltpu.roll(odd, COL_BLOCK, 0))
            tiles[(2 * i + 1) * pairs + u] = jnp.where(low, pltpu.roll(even, COL_BLOCK, 0), odd)
    return jnp.concatenate(tiles)


def scale_column(eig):
    modes = eig.shape[1]
    row = lax.broadcasted_iota(jnp.int32, (modes, modes), 0)
    column = lax.broadcasted_iota(jnp.int32, (modes, modes), 1)
    value = jnp.sum(jnp.where(row == column, eig, 0.0), axis=1, keepdims=True)
    return jnp.broadcast_to(lax.rsqrt(value), (modes, LANES))


def multiply_kernel(eig_ref, slab_ref, snap_ref, out_ref, scaled_ref):
    p, q = lax.axis_index("snap"), lax.axis_index("space")
    _, snap_count, _, chunk = slab_ref.shape
    outer_count = snap_count // GROUPS
    scale = scale_column(eig_ref[...])
    for outer in range(outer_count):
        for t in range(chunk // LANES):
            slots = [p ^ (outer * GROUPS + g) for g in range(GROUPS)]
            for j, block in enumerate(interleave([all_modes(slab_ref, q, slot, t) for slot in slots])):
                tile = (t * GROUPS + j) * outer_count + outer
                scaled_ref[:, tile * LANES : (tile + 1) * LANES] = (block * scale).astype(jnp.bfloat16)
    total = lax.dot_general(
        snap_ref[...], scaled_ref[...], (((1,), (1,)), ((), ())), preferred_element_type=jnp.float32
    ).T
    cells = out_ref.shape[2]
    for owner in range(snap_count):
        out_ref[p ^ owner] = total[:, owner * cells : (owner + 1) * cells]


def multiply(eig, slab, snapshots):
    space_count, snap_count, width, _ = slab.shape
    cells, depth = snapshots.shape
    modes = width * space_count
    out = (snap_count, modes, cells // snap_count)
    return pl.pallas_call(
        multiply_kernel,
        out_shape=jax.ShapeDtypeStruct(out, jnp.float32),
        in_specs=[IN_VMEM] * 3,
        out_specs=IN_VMEM,
        scratch_shapes=[pltpu.VMEM((modes, depth), jnp.bfloat16)],
        compiler_params=params(12),
        name="multiply",
    )(eig, slab, snapshots)


def pair_kernel(count, mine_ref, theirs_ref, *refs):
    held_refs, (coef_ref, next_ref, *sum_refs) = refs[:count], refs[count:]
    snap_count, modes, _ = mine_ref.shape
    sums = [mine_ref[s] + theirs_ref[s ^ 1] for s in range(snap_count)]
    held = [held_refs[s // 2][s % 2].astype(jnp.bfloat16) for s in range(snap_count)]
    wide = jnp.concatenate(sums, axis=1)
    high = wide.astype(jnp.bfloat16)
    low = (wide - high.astype(jnp.float32)).astype(jnp.bfloat16)
    both = jnp.dot(jnp.concatenate([high, low]), jnp.concatenate(held), preferred_element_type=jnp.float32)
    coef = both[:modes] + both[modes:]
    coef_ref[...] = coef
    next_ref[:, : coef.shape[1]] = coef
    next_ref[:, coef.shape[1] :] = sums[2]
    for sum_ref, d in zip(sum_refs, [0, *range(2, count)]):
        sum_ref[...] = sums[2 * d]


def pair(mine, theirs, held):
    _, modes, cells = mine.shape
    columns = held[0].shape[2]
    shapes = [(modes, columns), (modes, columns + cells)] + [(modes, cells)] * (len(held) - 1)
    return pl.pallas_call(
        lambda *refs: pair_kernel(len(held), *refs),
        out_shape=[jax.ShapeDtypeStruct(shape, jnp.float32) for shape in shapes],
        in_specs=[IN_VMEM] * (2 + len(held)),
        out_specs=[IN_VMEM] * len(shapes),
        compiler_params=params(6),
        name="pair",
    )(mine, theirs, *held)


def per_device(snapshots, vectors_cyclic, eigen_values, held_out):
    snap_count = lax.axis_size("snap")
    space_count = lax.axis_size("space")
    p = lax.axis_index("snap")
    chips = range(1, snap_count // 2)
    others = range(1, space_count)

    own = vectors_cyclic.T
    other = swap(own, "snap", 1)
    pieces = join(other, cut(own, snap_count))
    near = [pieces[0]] + [swap(pieces[d], "snap", 2 * d) for d in chips]

    first, second = jnp.concatenate(near[:2]), jnp.concatenate(near[2:])
    firsts = [first] + [swap(first, "space", e) for e in others]
    seconds = [second] + [swap(second, "space", e) for e in others]
    slab = jnp.stack([jnp.concatenate(parts) for parts in zip(firsts, seconds)])

    half = held_out.shape[1] // 2
    wide = held_out.astype(jnp.float32)
    held_keep = lax.dynamic_slice_in_dim(wide, (p & 1) * half, half, 1)
    held_send = lax.dynamic_slice_in_dim(wide, (1 - (p & 1)) * half, half, 1)
    held = jnp.stack([held_keep, swap(held_send, "snap", 1)])
    held = [held] + [swap(held, "snap", 2 * d) for d in chips]

    mine = multiply(eigen_values[None, :], slab, snapshots)
    coef, beside, *sums = pair(mine, swap(mine, "snap", 1), held)
    beside = swap(beside, "snap", 2)
    coef = tree_sum([coef, beside[:, :half]] + [swap(coef, "snap", 2 * d) for d in chips[1:]])
    terms = [sums[0], beside[:, half:]] + [swap(sums[d - 1], "snap", 2 * d) for d in chips[1:]]
    coef = tree_sum([coef] + [swap(coef, "space", e) for e in others])
    modes = tree_sum(lax.optimization_barrier((terms, coef))[0])
    far = swap(coef, "snap", 1)
    even = p % 2 == 0
    coefficients = jnp.concatenate([jnp.where(even, coef, far), jnp.where(even, far, coef)], axis=1)

    total_cells = snapshots.shape[0] * space_count
    return (modes.astype(jnp.bfloat16).T, coefficients / math.sqrt(total_cells))


def solution(mesh):
    return jax.shard_map(
        per_device,
        mesh=mesh,
        in_specs=(P("space", "snap"), P("snap", "space"), P(), P(("space", "snap"), None)),
        out_specs=(P(("space", "snap"), None), P()),
        check_vma=False,
    )
```
